32 devices in a mesh: row: 8 (over z, y), col: 4 (over x, core).
Axes of the slice: x: 2, y: 2, z: 4, core: 2. Of those that a mesh axis runs over, the one named last changes fastest.
Arguments:
- jacobian: float32 [16384, 16384], P('row', 'col'), may hold values from -6 to 6
- diff_inputs: float32 [32768, 128], P('row'), may hold values from -0.00390625 to 0.00390625
- diff_outputs: float32 [32768, 128], P('row'), may hold values from -6 to 6
- face_dof: int32 [32768], P('row'), may hold values from 0 to 16383, as said below
- counts: int32 [8], P('row'), may hold values from 128 to 4096, as said below
- residual: float32 [16384], P('col'), may hold values from -0.046875 to 0.046875
- trial: float32 [16384], P('row'), may hold values from -6 to 6
Outputs:
- updated: float32 [16384, 16384], P('row', 'col')
- corrected: float32 [16384], P('row')
The draws below stay inside these ranges and needn't reach their ends.
Inputs may be any that keep to these rules, and one draw needn't show every extreme that they name: Each owner's count is a multiple of 128; the counts sum to 16384; some owner holds exactly 4096. `face_dof`: live slots name every degree of freedom exactly once over all owners, in runs of 128 consecutive degrees of freedom starting at multiples of 128; slots at or past an owner's count hold arbitrary values that belong to no column.
All inputs are finite; a program needn't handle non-finite values. Where the reference program divides by a largest or mean magnitude, that divisor is 1e-20 or more.
Results may differ from the reference program's by a relative error of at most 0.0001.
Values sent between devices are 32-bit elements; how exact they have to be, the bound alone decides.
A program may use at most 192 MiB of HBM per device.

```python
import jax
import jax.numpy as jnp
from jax import lax

M = 16384
K = 128
UNIT = 128
NS = 4
CAP = 4096
N_ROW = 8


def owner_layout(key):
    base = jax.random.fold_in(key, 7)
    key_big, key_fill, key_perm, key_junk = jax.random.split(base, 4)
    units_total = M // UNIT
    most_units = 2 * (units_total // N_ROW)
    biggest = jax.random.randint(key_big, (), 0, N_ROW)
    units = jnp.ones((N_ROW,), jnp.int32).at[biggest].set(most_units)
    remain = units_total - N_ROW - (most_units - 1)

    def add_unit(index, units_now):
        scores = jax.random.randint(jax.random.fold_in(key_fill, index), (N_ROW,), 0, 1 << 20) * N_ROW
        scores = scores + jnp.arange(N_ROW, dtype=jnp.int32)
        scores = jnp.where(units_now >= most_units, -1, scores)
        return units_now.at[jnp.argmax(scores)].add(1)
    units = lax.fori_loop(0, remain, add_unit, units)
    order = jax.random.permutation(key_perm, units_total).astype(jnp.int32)
    starts = jnp.cumsum(units) - units
    slots = jnp.arange(CAP, dtype=jnp.int32)
    live = slots[None, :] < (units * UNIT)[:, None]
    block_index = jnp.clip(starts[:, None] + slots[None, :] // UNIT, 0, units_total - 1)
    dofs = order[block_index] * UNIT + slots[None, :] % UNIT
    junk = jax.random.randint(key_junk, (N_ROW, CAP), 0, M)
    mapped = jnp.where(live, dofs, junk).reshape(-1).astype(jnp.int32)
    return ((units * UNIT).astype(jnp.int32), mapped)


def draw_counts(key, part):
    return owner_layout(key)[0]


def draw_face_dof(key, part):
    return owner_layout(key)[1]


def levels(rng, shape, cuts, smallest, top_value):
    gain, own = 1.0, jax.random.fold_in(rng, 6)
    for dim, blocks in cuts:
        steps = jnp.exp(jax.random.uniform(jax.random.fold_in(own, dim), (blocks,), jnp.float32, smallest / len(cuts), top_value / len(cuts)))
        gain = gain * jnp.repeat(steps, shape[dim] // blocks).reshape([-1 if axis == dim else 1 for axis in range(len(shape))])
    return gain


def gaussian(key, dims, spread, limit, cuts=(), held_as=jnp.bfloat16):
    array = jax.random.normal(key, dims, jnp.float32) * spread
    if len(cuts) > 0:
        array = levels(key, dims, cuts, -0.22, 0.18) * array
    return jnp.clip(array, min=-limit, max=limit).astype(held_as)


def setup_inputs(seed: int = 0) -> dict:
    seeds = jax.random.split(jax.random.key(seed), 8)
    return {
        "jacobian": gaussian(seeds[0], (M, M), 1.0, 6.0, ((0, 8), (1, 4)), jnp.float32),
        "diff_inputs": gaussian(seeds[1], (N_ROW * CAP, K), (M * M // K) ** -0.5, 0.00390625, ((0, 8),), jnp.float32),
        "diff_outputs": gaussian(seeds[2], (N_ROW * CAP, K), 1.0, 6.0, ((0, 8),), jnp.float32),
        "face_dof": draw_face_dof(jax.random.fold_in(seeds[7], 71), 0),
        "counts": draw_counts(jax.random.fold_in(seeds[7], 71), 0),
        "residual": gaussian(seeds[5], (M,), M ** -0.5, 0.046875, ((0, 4),), jnp.float32),
        "trial": gaussian(seeds[6], (M,), 1.0, 6.0, ((0, 8),), jnp.float32),
    }


HIGH = lax.Precision.HIGHEST
REG = 0.1


def ns_inverse(gram):
    eye = jnp.eye(K, dtype=jnp.float32)
    regular = gram + REG * (jnp.trace(gram) / K) * eye
    norm_one = jnp.max(jnp.sum(jnp.abs(regular), axis=0))
    iterate = regular / (norm_one * norm_one)
    for sweep in range(NS):
        iterate = jnp.dot(iterate, 2.0 * eye - jnp.dot(regular, iterate, precision=HIGH), precision=HIGH)
    return iterate


def reference(jacobian, diff_inputs, diff_outputs, face_dof, counts, residual, trial):
    slots = jnp.arange(N_ROW * CAP, dtype=jnp.int32)
    owner = slots // CAP
    live = (slots % CAP) < counts[owner]
    masked = jnp.where(live[:, None], diff_inputs, 0.0)
    gram = jnp.dot(masked.T, masked, precision=HIGH)
    target = jnp.where(live, face_dof, M).astype(jnp.int32)
    inverse = jnp.zeros((M + 1,), jnp.int32).at[target].set(slots)[:M]
    v_full = diff_inputs[inverse]
    w_full = diff_outputs[inverse]
    j_times_v = jnp.dot(jacobian, v_full, precision=HIGH)
    diff = w_full - j_times_v
    zmat = ns_inverse(gram)
    updated = jacobian + jnp.dot(jnp.dot(diff, zmat, precision=HIGH), v_full.T, precision=HIGH)
    corrected = trial - jnp.dot(updated, residual, precision=HIGH)
    return updated, corrected
```

```python
import functools

import jax
import jax.numpy as jnp
from jax import lax
from jax.experimental import pallas as pl
from jax.experimental.pallas import tpu as pltpu
from jax.sharding import PartitionSpec as P

K = 128
NS = 4
UNIT = 128
TILE = 256

HIGH = lax.Precision.HIGHEST
REG = 0.1
F32 = jnp.float32
BF16 = jnp.bfloat16
MESH = pl.DeviceIdType.MESH
VMEM_SPEC = pl.BlockSpec(memory_space=pltpu.VMEM)
SMEM_SPEC = pl.BlockSpec(memory_space=pltpu.SMEM)


def ns_inverse(gram):
    eye = jnp.eye(K, dtype=F32)
    regular = gram + REG * (jnp.trace(gram) / K) * eye
    norm_one = jnp.max(jnp.sum(jnp.abs(regular), axis=0))
    iterate = regular / (norm_one * norm_one)
    for sweep in range(NS):
        iterate = jnp.dot(
            iterate, 2.0 * eye - jnp.dot(regular, iterate, precision=HIGH), precision=HIGH
        )
    return iterate


def split(x):
    hi = x.astype(BF16)
    return hi, (x - hi.astype(F32)).astype(BF16)


def ring_place(index, n):
    return index // 2 + (index % 2) * (n - 1 - 2 * (index // 2))


def ring_index(place, n):
    side = place // (n // 2)
    level = place + side * (n - 1 - 2 * place)
    return 2 * level + side


def ring_kernel(n, parts, src_ref, mask_ref, x_ref, out_ref, landed, sent, send_sem, recv_sem):
    place = ring_place(lax.axis_index("row"), n)
    right = ring_index((place + 1) % n, n)
    left = ring_index((place + n - 1) % n, n)
    barrier = pltpu.get_barrier_semaphore()
    for peer in (left, right):
        pl.semaphore_signal(barrier, inc=1, device_id={"row": peer}, device_id_type=MESH)
    pl.semaphore_wait(barrier, 2)

    def granule(way, back, part):
        sign = 1 if way == 0 else -1
        chunk = (place + 2 * n - sign * back) % n
        return (way * n + chunk) * parts + part

    def own(at):
        return x_ref[src_ref[at]] * mask_ref[at]

    def copy(step, way, part, source, target):
        return pltpu.make_async_remote_copy(
            src_ref=source,
            dst_ref=target,
            send_sem=send_sem.at[way, step, part],
            recv_sem=recv_sem.at[way, step, part],
            device_id={"row": right if way == 0 else left},
            device_id_type=MESH,
        )

    copies = {}
    last = 2 * (n - 1)
    for step in range(last + 1):
        for part in range(parts):
            for way in range(2):
                if step > 0:
                    copies[step - 1, way, part].wait_recv()
                if step < n - 1:
                    at = granule(way, step, part)
                    value = own(at)
                    if step > 0:
                        value = value + landed[way, step - 1, part]
                    sent[way, step, part] = value
                    source, target = sent.at[way, step, part], landed.at[way, step, part]
                elif step < last:
                    at = granule(way, step, part)
                    if step == n - 1:
                        out_ref[at] = own(at) + landed[way, step - 1, part]
                    source, target = out_ref.at[at], out_ref.at[at]
                else:
                    continue
                copies[step, way, part] = copy(step, way, part, source, target)
                copies[step, way, part].start()
    for key in copies:
        copies[key].wait_send()


def ring_sum(src, mask, x, rows, n):
    chunk = rows // (2 * n)
    part = min(UNIT, chunk)
    parts = chunk // part
    granules = rows // part
    return pl.pallas_call(
        functools.partial(ring_kernel, n, parts),
        out_shape=jax.ShapeDtypeStruct((granules, part, K), F32),
        in_specs=[SMEM_SPEC, SMEM_SPEC, VMEM_SPEC],
        out_specs=VMEM_SPEC,
        scratch_shapes=[
            pltpu.VMEM((2, n - 1, parts, part, K), F32),
            pltpu.VMEM((2, n - 1, parts, part, K), F32),
            pltpu.SemaphoreType.DMA((2, 2 * (n - 1), parts)),
            pltpu.SemaphoreType.DMA((2, 2 * (n - 1), parts)),
        ],
        compiler_params=pltpu.CompilerParams(collective_id=0, has_side_effects=True),
    )(src, mask, x.reshape(-1, part, K)).reshape(rows, K)


def lookup(run_unit, wanted):
    hit = run_unit[None, :] == wanted[:, None]
    src = jnp.sum(jnp.where(hit, jnp.arange(run_unit.shape[0], dtype=jnp.int32)[None, :], 0), axis=1)
    return src.astype(jnp.int32), jnp.any(hit, axis=1).astype(F32)


def place_kernel(src_ref, mask_ref, x_ref, out_ref):
    for unit in range(out_ref.shape[0]):
        out_ref[unit] = x_ref[src_ref[unit]] * mask_ref[unit]


def place_units(src, mask, x):
    return pl.pallas_call(
        place_kernel,
        out_shape=jax.ShapeDtypeStruct((src.shape[0], UNIT, K), F32),
        in_specs=[SMEM_SPEC, SMEM_SPEC, VMEM_SPEC],
        out_specs=VMEM_SPEC,
    )(src, mask, x.reshape(-1, UNIT, K)).reshape(-1, K)


def product_kernel(j_ref, v_ref, r_ref, jv_ref, jr_ref, gram_ref, beta_ref, vb):
    @pl.when(pl.program_id(0) == 0)
    def _():
        hi, lo = split(v_ref[...])
        vb[:, :K] = hi
        vb[:, K:] = lo
        both = vb[...]
        full = lax.dot_general(both, both, (((0,), (0,)), ((), ())), preferred_element_type=F32)
        gram_ref[...] = full[:K, :K] + (full[:K, K:] + full[K:, :K]) + full[K:, K:]
        rows = jnp.broadcast_to(r_ref[...], (8, r_ref.shape[1]))
        r_hi, r_lo = split(rows)
        b_hi = jnp.dot(r_hi, both, preferred_element_type=F32)
        b_lo = jnp.dot(r_lo, both, preferred_element_type=F32)
        beta_ref[...] = b_hi[:, :K] + (b_hi[:, K:] + b_lo[:, :K])

    tile = j_ref[...]
    hi, lo = split(tile)
    main = jnp.dot(hi, vb[...], preferred_element_type=F32)
    rest = jnp.dot(lo, vb[:, :K], preferred_element_type=F32)
    jv_ref[...] = main[:, :K] + (main[:, K:] + rest)
    total = jnp.zeros((tile.shape[0], K), F32)
    for at in range(0, tile.shape[1], K):
        total = total + j_ref[:, at : at + K] * r_ref[:, at : at + K]
    jr_ref[...] = jnp.sum(jnp.transpose(total), axis=0, keepdims=True)


def products(jacobian, v_cols, residual):
    rows, cols = jacobian.shape
    return pl.pallas_call(
        product_kernel,
        grid=(rows // TILE,),
        out_shape=(
            jax.ShapeDtypeStruct((rows, K), F32),
            jax.ShapeDtypeStruct((1, rows), F32),
            jax.ShapeDtypeStruct((K, K), F32),
            jax.ShapeDtypeStruct((8, K), F32),
        ),
        in_specs=[
            pl.BlockSpec((TILE, cols), lambda i: (i, 0)),
            pl.BlockSpec((cols, K), lambda i: (0, 0)),
            pl.BlockSpec((1, cols), lambda i: (0, 0)),
        ],
        out_specs=(
            pl.BlockSpec((TILE, K), lambda i: (i, 0)),
            pl.BlockSpec((1, TILE), lambda i: (0, i)),
            pl.BlockSpec((K, K), lambda i: (0, 0)),
            pl.BlockSpec((8, K), lambda i: (0, 0)),
        ),
        scratch_shapes=[pltpu.VMEM((cols, 2 * K), BF16)],
    )(jacobian, v_cols, residual.reshape(1, cols))


def update_kernel(j_ref, u_ref, vt_ref, out_ref):
    hi, lo = split(u_ref[...])
    twice = jnp.concatenate([hi, hi], axis=1)
    main = jnp.dot(twice, vt_ref[...], preferred_element_type=F32)
    rest = jnp.dot(lo, vt_ref[:K, :], preferred_element_type=F32)
    out_ref[...] = j_ref[...] + (main + rest)


def update(jacobian, u_rows, vt):
    rows, cols = jacobian.shape
    return pl.pallas_call(
        update_kernel,
        grid=(rows // TILE,),
        out_shape=jax.ShapeDtypeStruct((rows, cols), F32),
        in_specs=[
            pl.BlockSpec((TILE, cols), lambda i: (i, 0)),
            pl.BlockSpec((TILE, K), lambda i: (i, 0)),
            pl.BlockSpec((2 * K, cols), lambda i: (0, 0)),
        ],
        out_specs=pl.BlockSpec((TILE, cols), lambda i: (i, 0)),
    )(jacobian, u_rows, vt)


def per_device(jacobian, diff_inputs, diff_outputs, face_dof, counts, residual, trial):
    row_block, col_block = jacobian.shape
    n_row, n_col = lax.axis_size("row"), lax.axis_size("col")
    col_at = lax.axis_index("col")
    runs = face_dof.shape[0] // UNIT
    first = jnp.arange(runs, dtype=jnp.int32) * UNIT
    run_unit = jnp.where(first < counts[0], face_dof.reshape(runs, UNIT)[:, 0] // UNIT, -1)

    part = min(UNIT, col_block // (2 * n_row))
    per_unit = UNIT // part
    granule = jnp.arange(col_block // part, dtype=jnp.int32)
    v_src, v_mask = lookup(run_unit, col_at * (col_block // UNIT) + granule // per_unit)
    v_src = v_src * per_unit + granule % per_unit
    v_cols = ring_sum(v_src, v_mask, diff_inputs, col_block, n_row)

    share = row_block // n_col // UNIT
    unit = jnp.arange(n_row * share, dtype=jnp.int32)
    w_unit = (unit // share) * (row_block // UNIT) + col_at * share + unit % share
    w_src, w_mask = lookup(run_unit, w_unit)
    w_piece = place_units(w_src, w_mask, diff_outputs)
    w_rows = lax.psum_scatter(w_piece, "row", scatter_dimension=0, tiled=True)

    jv_part, jr_part, gram_part, beta_part = products(jacobian, v_cols, residual)
    jv_rows = lax.psum_scatter(jv_part, "col", scatter_dimension=0, tiled=True)
    gram, beta, j_r = lax.psum((gram_part, beta_part, jr_part), "col")
    zmat = ns_inverse(gram)
    u_share = jnp.dot(w_rows - jv_rows, zmat, precision=HIGH)
    u_rows = lax.all_gather(u_share, "col", axis=0, tiled=True)
    v_t = v_cols.T
    vt_hi = lax.reduce_precision(v_t, 8, 7)
    vt = jnp.concatenate([vt_hi.astype(BF16), (v_t - vt_hi).astype(BF16)], axis=0)
    updated = update(jacobian, u_rows, vt)
    corrected = trial - (j_r[0] + jnp.dot(u_rows, beta[0], precision=HIGH))
    return (updated, corrected)


def solution(mesh):
    placed = (
        P("row", "col"),
        P("row", None),
        P("row", None),
        P("row"),
        P("row"),
        P("col"),
        P("row"),
    )
    return jax.shard_map(
        per_device,
        mesh=mesh,
        in_specs=placed,
        out_specs=(P("row", "col"), P("row")),
        check_vma=False,
    )
```

```python
import functools

import jax
import jax.numpy as jnp
from jax import lax
from jax.experimental import pallas as pl
from jax.experimental.pallas import tpu as pltpu
from jax.sharding import PartitionSpec as P

K = 128
NS = 4
UNIT = 128
TILE = 256

HIGH = lax.Precision.HIGHEST
REG = 0.1
F32 = jnp.float32
BF16 = jnp.bfloat16
MESH = pl.DeviceIdType.MESH
VMEM_SPEC = pl.BlockSpec(memory_space=pltpu.VMEM)
SMEM_SPEC = pl.BlockSpec(memory_space=pltpu.SMEM)


def split(x):
    hi = x.astype(BF16)
    return hi, (x - hi.astype(F32)).astype(BF16)


def ring_place(index, n):
    return index // 2 + (index % 2) * (n - 1 - 2 * (index // 2))


def ring_index(place, n):
    side = place // (n // 2)
    level = place + side * (n - 1 - 2 * place)
    return 2 * level + side


def ring_kernel(
    n, parts, src_ref, mask_ref, x_ref, r_ref, vb_ref, vt_ref, gb_ref,
    whole, landed, sent, gram, beta, send_sem, recv_sem,
):
    place = ring_place(lax.axis_index("row"), n)
    right = ring_index((place + 1) % n, n)
    left = ring_index((place + n - 1) % n, n)
    barrier = pltpu.get_barrier_semaphore()
    for peer in (left, right):
        pl.semaphore_signal(barrier, inc=1, device_id={"row": peer}, device_id_type=MESH)
    pl.semaphore_wait(barrier, 2)

    def granule(way, back, part):
        sign = 1 if way == 0 else -1
        chunk = (place + 2 * n - sign * back) % n
        return (way * n + chunk) * parts + part

    def own(at):
        return x_ref[src_ref[at]] * mask_ref[at]

    def copy(step, way, part, source, target):
        return pltpu.make_async_remote_copy(
            src_ref=source,
            dst_ref=target,
            send_sem=send_sem.at[way, step, part],
            recv_sem=recv_sem.at[way, step, part],
            device_id={"row": right if way == 0 else left},
            device_id_type=MESH,
        )

    per_unit = UNIT // whole.shape[1]

    def absorb(unit):
        rows = jnp.concatenate([whole[unit * per_unit + sub] for sub in range(per_unit)], axis=0)
        at = pl.ds(pl.multiple_of(unit * UNIT, UNIT), UNIT)
        hi, lo = split(rows)
        both = jnp.concatenate([hi, lo], axis=1)
        vb_ref[at, :] = both
        t_hi, t_lo = split(jnp.transpose(rows))
        vt_ref[:K, at] = t_hi
        vt_ref[K:, at] = t_lo
        gram[...] += lax.dot_general(
            both, both, (((0,), (0,)), ((), ())), preferred_element_type=F32
        )
        r_hi, r_lo = split(jnp.broadcast_to(r_ref[:, at], (8, UNIT)))
        beta[...] += jnp.dot(
            jnp.concatenate([r_hi, r_lo], axis=0), both, preferred_element_type=F32
        )

    gram[...] = jnp.zeros_like(gram)
    beta[...] = jnp.zeros_like(beta)
    copies = {}
    last = 2 * (n - 1)
    for step in range(last + 1):
        for part in range(parts):
            for way in range(2):
                if step > 0:
                    copies[step - 1, way, part].wait_recv()
                at = granule(way, step, part)
                if step < n - 1:
                    value = own(at)
                    if step > 0:
                        value = value + landed[way, step - 1, part]
                    sent[way, step, part] = value
                    source, target = sent.at[way, step, part], landed.at[way, step, part]
                else:
                    if step == n - 1:
                        whole[at] = own(at) + landed[way, step - 1, part]
                    source, target = whole.at[at], whole.at[at]
                if step < last:
                    copies[step, way, part] = copy(step, way, part, source, target)
                    copies[step, way, part].start()
                if step >= n - 1 and per_unit == 1:
                    absorb(at)
    if per_unit > 1:
        for unit in range(whole.shape[0] // per_unit):
            absorb(unit)
    gb_ref[:K, :] = gram[:K, :K] + (gram[:K, K:] + gram[K:, :K]) + gram[K:, K:]
    gb_ref[K:, :] = beta[:8, :K] + (beta[:8, K:] + beta[8:, :K])
    for key in copies:
        copies[key].wait_send()


def ring_sum(src, mask, x, residual, rows, n):
    chunk = rows // (2 * n)
    part = min(UNIT, chunk)
    parts = chunk // part
    return pl.pallas_call(
        functools.partial(ring_kernel, n, parts),
        out_shape=(
            jax.ShapeDtypeStruct((rows, 2 * K), BF16),
            jax.ShapeDtypeStruct((2 * K, rows), BF16),
            jax.ShapeDtypeStruct((K + 8, K), F32),
        ),
        in_specs=[SMEM_SPEC, SMEM_SPEC, VMEM_SPEC, VMEM_SPEC],
        out_specs=(VMEM_SPEC, VMEM_SPEC, VMEM_SPEC),
        scratch_shapes=[
            pltpu.VMEM((rows // part, part, K), F32),
            pltpu.VMEM((2, n - 1, parts, part, K), F32),
            pltpu.VMEM((2, n - 1, parts, part, K), F32),
            pltpu.VMEM((2 * K, 2 * K), F32),
            pltpu.VMEM((16, 2 * K), F32),
            pltpu.SemaphoreType.DMA((2, 2 * (n - 1), parts)),
            pltpu.SemaphoreType.DMA((2, 2 * (n - 1), parts)),
        ],
        compiler_params=pltpu.CompilerParams(collective_id=0, has_side_effects=True),
    )(src, mask, x.reshape(-1, part, K), residual)


def lookup(run_unit, wanted):
    hit = run_unit[None, :] == wanted[:, None]
    src = jnp.sum(jnp.where(hit, jnp.arange(run_unit.shape[0], dtype=jnp.int32)[None, :], 0), axis=1)
    return src.astype(jnp.int32), jnp.any(hit, axis=1).astype(F32)


def product_kernel(
    n, nc, parts, src_ref, mask_ref, x_ref, gb_ref, r_ref, vb_ref, j_ref,
    u_ref, beta_ref, jr_ref,
    w_land, w_sent, w_share, jv, jv_land, jr_all, gb_all, u_all,
    w_send, w_recv, jv_send, jv_recv, gb_send, gb_recv, jr_send, jr_recv, u_send, u_recv,
):
    tiles = jr_all.shape[1]
    tile = jr_all.shape[2]
    share = jv_land.shape[1]
    per_share = share // tile
    grain = w_share.shape[2]
    step_now = pl.program_id(0)
    me = lax.axis_index("col")
    place = ring_place(lax.axis_index("row"), n)
    right = ring_index((place + 1) % n, n)
    left = ring_index((place + n - 1) % n, n)
    peers = [(me + k) % nc for k in range(1, nc)]

    def to_col(source, target, send, recv, peer):
        return pltpu.make_async_remote_copy(
            src_ref=source, dst_ref=target, send_sem=send, recv_sem=recv,
            device_id={"col": peer}, device_id_type=MESH,
        )

    def gb_copy(k, slot):
        return to_col(gb_ref, gb_all.at[slot], gb_send.at[k], gb_recv.at[slot], peers[k])

    def jr_copy(k, slot):
        return to_col(jr_all.at[slot], jr_all.at[slot], jr_send.at[k], jr_recv.at[slot], peers[k])

    def jv_copy(at, sender, owner):
        rows = pl.ds(pl.multiple_of((at % per_share) * tile, tile), tile)
        return to_col(
            jv.at[at], jv_land.at[sender, rows], jv_send.at[at],
            jv_recv.at[sender, at % per_share], owner,
        )

    def w_copy(step, way, part):
        return pltpu.make_async_remote_copy(
            src_ref=w_sent.at[way, step, part], dst_ref=w_land.at[way, step, part],
            send_sem=w_send.at[way, step, part], recv_sem=w_recv.at[way, step, part],
            device_id={"row": right if way == 0 else left}, device_id_type=MESH,
        )

    def w_step(step):
        for part in range(parts):
            for way in range(2):
                sign = 1 if way == 0 else -1
                block = ring_index((place + 2 * n - sign * (step + 1)) % n, n)
                at = (block * 2 + way) * parts + part
                value = x_ref[src_ref[at]] * mask_ref[at]
                if step > 0:
                    w_copy(step - 1, way, part).wait_recv()
                    value = value + w_land[way, step - 1, part]
                if step < n - 1:
                    w_sent[way, step, part] = value
                    w_copy(step, way, part).start()
                else:
                    w_share[way, part] = value

    @pl.when(step_now == 0)
    def _():
        barrier = pltpu.get_barrier_semaphore()
        for peer in (left, right):
            pl.semaphore_signal(barrier, inc=1, device_id={"row": peer}, device_id_type=MESH)
        for peer in peers:
            pl.semaphore_signal(barrier, inc=1, device_id={"col": peer}, device_id_type=MESH)
        pl.semaphore_wait(barrier, 2 + len(peers))
        gb_all[me] = gb_ref[...]
        for k in range(nc - 1):
            gb_copy(k, me).start()

    each = -(-n // tiles)
    for at in range(tiles):
        @pl.when(step_now == at)
        def _():
            for step in range(at * each, min(n, (at + 1) * each)):
                w_step(step)

    hi, lo = split(j_ref[...])
    both = jnp.dot(jnp.concatenate([hi, lo], axis=0), vb_ref[...], preferred_element_type=F32)
    jv_tile = both[:tile, :K] + (both[:tile, K:] + both[tile:, :K]) + both[tile:, K:]
    total = jnp.zeros((tile, K), F32)
    for at in range(0, j_ref.shape[1], K):
        total = total + j_ref[:, at : at + K] * r_ref[:, at : at + K]
    jr_all[me, pl.ds(step_now, 1), :] = jnp.sum(jnp.transpose(total), axis=0, keepdims=True)
    jv[step_now] = jv_tile
    owner = step_now // per_share

    @pl.when(owner != me)
    def _():
        jv_copy(step_now, me, owner).start()

    @pl.when(owner == me)
    def _():
        rows = pl.ds(pl.multiple_of((step_now % per_share) * tile, tile), tile)
        jv_land[me, rows] = jv_tile

    @pl.when(step_now == tiles - 1)
    def _():
        for k in range(nc - 1):
            jr_copy(k, me).start()
        for k in range(nc - 1):
            gb_copy(k, peers[k]).wait_recv()
        sums = gb_all[0]
        for slot in range(1, nc):
            sums = sums + gb_all[slot]
        beta_ref[...] = sums[K:]
        gram = sums[:K]
        eye = (
            lax.broadcasted_iota(jnp.int32, (K, K), 0) == lax.broadcasted_iota(jnp.int32, (K, K), 1)
        ).astype(F32)
        trace = jnp.sum(jnp.sum(gram * eye, axis=0, keepdims=True), axis=1, keepdims=True)
        regular = gram + REG * (trace / K) * eye
        norm_one = jnp.max(
            jnp.sum(jnp.abs(regular), axis=0, keepdims=True), axis=1, keepdims=True
        )
        zmat = regular / (norm_one * norm_one)
        for sweep in range(NS):
            inner = jnp.dot(regular, zmat, precision=HIGH, preferred_element_type=F32)
            zmat = jnp.dot(zmat, 2.0 * eye - inner, precision=HIGH, preferred_element_type=F32)

        for k in range(nc - 1):
            for at in range(per_share):
                jv_copy(at, peers[k], me).wait_recv()
        for way in range(2):
            for part in range(parts):
                at = (way * parts + part) * grain
                jv_sum = jnp.zeros((grain, K), F32)
                for slot in range(nc):
                    jv_sum = jv_sum + jv_land[slot, at : at + grain]
                u_all[me, at : at + grain] = jnp.dot(
                    w_share[way, part] - jv_sum, zmat, precision=HIGH, preferred_element_type=F32
                )

        partner = me + 1 - 2 * (me % 2)

        def u_copy(slot, hop, peer):
            return to_col(
                u_all.at[slot], u_all.at[slot], u_send.at[hop], u_recv.at[slot], peer
            )

        half = nc // 2
        far = [(me + 2 * k) % nc for k in range(1, half)]
        for k, peer in enumerate(far):
            u_copy(me, k, peer).start()
        u_copy(me, half - 1, partner).start()
        for k in range(1, half):
            slot = (me + 2 * k) % nc
            u_copy(slot, half - 1 + k, partner).wait_recv()
            u_copy(slot, half - 1 + k, partner).start()

        for k in range(nc - 1):
            jr_copy(k, peers[k]).wait_recv()
        jr_sum = jr_all[0]
        for slot in range(1, nc):
            jr_sum = jr_sum + jr_all[slot]
        jr_ref[...] = jr_sum

        for k in range(half):
            slot = (partner + 2 * k) % nc
            u_copy(slot, 0, partner).wait_recv()
        u_ref[...] = u_all[...]
        for hop in range(nc - 1):
            u_copy(me, hop, partner).wait_send()
        for k in range(nc - 1):
            gb_copy(k, me).wait_send()
            jr_copy(k, me).wait_send()
            for at in range(per_share):
                jv_copy(peers[k] * per_share + at, me, peers[k]).wait_send()
        for step in range(n - 1):
            for part in range(parts):
                for way in range(2):
                    w_copy(step, way, part).wait_send()


def products(jacobian, vb, gb, residual, src, mask, x, grain, n, nc):
    rows, cols = jacobian.shape
    share = rows // nc
    tile = min(TILE, share)
    tiles = rows // tile
    parts = share // (2 * grain)
    dma = pltpu.SemaphoreType.DMA
    whole = lambda shape: pl.BlockSpec(shape, lambda i: (0,) * len(shape))
    out_shape = (
        jax.ShapeDtypeStruct((nc, share, K), F32),
        jax.ShapeDtypeStruct((8, K), F32),
        jax.ShapeDtypeStruct((tiles, tile), F32),
    )
    return pl.pallas_call(
        functools.partial(product_kernel, n, nc, parts),
        grid=(tiles,),
        out_shape=out_shape,
        in_specs=[
            SMEM_SPEC, SMEM_SPEC, VMEM_SPEC, VMEM_SPEC, VMEM_SPEC, VMEM_SPEC,
            pl.BlockSpec((tile, cols), lambda i: (i, 0)),
        ],
        out_specs=(VMEM_SPEC, VMEM_SPEC, VMEM_SPEC),
        scratch_shapes=[
            pltpu.VMEM((2, n - 1, parts, grain, K), F32),
            pltpu.VMEM((2, n - 1, parts, grain, K), F32),
            pltpu.VMEM((2, parts, grain, K), F32),
            pltpu.VMEM((tiles, tile, K), F32),
            pltpu.VMEM((nc, share, K), F32),
            pltpu.VMEM((nc, tiles, tile), F32),
            pltpu.VMEM((nc, K + 8, K), F32),
            pltpu.VMEM((nc, share, K), F32),
            dma((2, n - 1, parts)), dma((2, n - 1, parts)),
            dma((tiles,)), dma((nc, share // tile)),
            dma((nc - 1,)), dma((nc,)), dma((nc - 1,)), dma((nc,)),
            dma((nc - 1,)), dma((nc,)),
        ],
        compiler_params=pltpu.CompilerParams(collective_id=1, has_side_effects=True),
    )(src, mask, x.reshape(-1, grain, K), gb, residual, vb, jacobian)


def update_kernel(j_ref, u_ref, vt_ref, beta_ref, jr_ref, trial_ref, out_ref, corrected_ref):
    hi, lo = split(u_ref[...])
    twice = jnp.concatenate([hi, hi], axis=1)
    main = jnp.dot(twice, vt_ref[...], preferred_element_type=F32)
    rest = jnp.dot(lo, vt_ref[:K, :], preferred_element_type=F32)
    out_ref[...] = j_ref[...] + (main + rest)
    low_rank = jnp.sum(jnp.transpose(u_ref[...] * beta_ref[:1]), axis=0, keepdims=True)
    corrected_ref[...] = trial_ref[...] - (jr_ref[...] + low_rank)


def update(jacobian, u_rows, vt, beta, j_r, trial):
    rows, cols = jacobian.shape
    row = pl.BlockSpec((1, TILE), lambda i: (0, i))
    return pl.pallas_call(
        update_kernel,
        grid=(rows // TILE,),
        out_shape=(
            jax.ShapeDtypeStruct((rows, cols), F32),
            jax.ShapeDtypeStruct((1, rows), F32),
        ),
        in_specs=[
            pl.BlockSpec((TILE, cols), lambda i: (i, 0)),
            pl.BlockSpec((TILE, K), lambda i: (i, 0)),
            pl.BlockSpec((2 * K, cols), lambda i: (0, 0)),
            pl.BlockSpec((8, K), lambda i: (0, 0)),
            row,
            row,
        ],
        out_specs=(pl.BlockSpec((TILE, cols), lambda i: (i, 0)), row),
    )(jacobian, u_rows, vt, beta, j_r, trial)


def per_device(jacobian, diff_inputs, diff_outputs, face_dof, counts, residual, trial):
    row_block, col_block = jacobian.shape
    n_row, n_col = lax.axis_size("row"), lax.axis_size("col")
    col_at = lax.axis_index("col")
    runs = face_dof.shape[0] // UNIT
    first = jnp.arange(runs, dtype=jnp.int32) * UNIT
    run_unit = jnp.where(first < counts[0], face_dof.reshape(runs, UNIT)[:, 0] // UNIT, -1)

    part = min(UNIT, col_block // (2 * n_row))
    per_unit = UNIT // part
    granule = jnp.arange(col_block // part, dtype=jnp.int32)
    v_src, v_mask = lookup(run_unit, col_at * (col_block // UNIT) + granule // per_unit)
    v_src = v_src * per_unit + granule % per_unit

    share = row_block // n_col
    grain = min(UNIT, share // 2)
    per_share = share // grain
    piece = jnp.arange(n_row * per_share, dtype=jnp.int32)
    w_row = (piece // per_share) * row_block + col_at * share + (piece % per_share) * grain
    w_src, w_mask = lookup(run_unit, w_row // UNIT)
    w_src = w_src * (UNIT // grain) + (w_row % UNIT) // grain

    r_row = residual.reshape(1, col_block)
    vb, vt, gb = ring_sum(v_src, v_mask, diff_inputs, r_row, col_block, n_row)
    u, beta, j_r = products(
        jacobian, vb, gb, r_row, w_src, w_mask, diff_outputs, grain, n_row, n_col
    )
    updated, corrected = update(
        jacobian, u.reshape(row_block, K), vt, beta,
        j_r.reshape(1, row_block), trial.reshape(1, row_block),
    )
    return (updated, corrected[0])


def solution(mesh):
    placed = (
        P("row", "col"),
        P("row", None),
        P("row", None),
        P("row"),
        P("row"),
        P("col"),
        P("row"),
    )
    return jax.shard_map(
        per_device,
        mesh=mesh,
        in_specs=placed,
        out_specs=(P("row", "col"), P("row")),
        check_vma=False,
    )
```
